32 devices in a mesh: clips: 2 (over y), ha: 8 (over z, x), wa: 2 (over core).
Axes of the slice: x: 2, y: 2, z: 4, core: 2. Of those that a mesh axis runs over, the one named last changes fastest.
Arguments:
- tokens: bfloat16 [5120, 5120], P(('clips', 'ha', 'wa')), parts along dimension 0, may hold values from -640 to 640
- timestep: int32 [2], P('clips'), parts along dimension 0, may hold values from 0 to 49
- time_table: float32 [50, 5120], replicated, may hold values from -3 to 3
- modulation: float32 [2, 5120], replicated, may hold values from -3 to 3
- head_weight: bfloat16 [5120, 64], replicated, may hold values from -0.078125 to 0.078125
- head_bias: float32 [64], replicated, may hold values from -3 to 3
- latent_std: float32 [16], replicated, may hold values from 0.5 to 2
- latent_mean: float32 [16], replicated, may hold values from -3 to 3
- conv_in_weight: bfloat16 [432, 384], replicated, may hold values from -0.3125 to 0.3125
- conv_in_bias: float32 [384], replicated, may hold values from -3 to 3
- norm_gain: float32 [384], replicated, may hold values from 0.1 to 1.9
- conv_weight: bfloat16 [10368, 384], P(None, 'wa'), may hold values from -0.0625 to 0.0625
- conv_bias: float32 [384], replicated, may hold values from -3 to 3
Outputs:
- block_input: bfloat16 [8, 16, 160, 384], P('clips', 'ha', 'wa'), parts along dimension 0
- block_mid: bfloat16 [8, 16, 160, 384], P('clips', 'ha', 'wa'), parts along dimension 0
The draws below stay inside these ranges and needn't reach their ends.
There are 2 independent parts, one for each index of `clips`. The reference program is written for one: setup_inputs(seed, part) draws one part's arguments, and reference() takes and returns one part's arrays. A program takes and returns all parts, laid end to end along the dimension named above; an argument that names none is the same for every part. Nothing has to cross between parts.
All inputs are finite; a program needn't handle non-finite values.
Results may differ from the reference program's by a relative error of at most 0.0058.
Values may be sent and summed in bfloat16 or wider, within the bound.
A program may use at most 128 MiB of HBM per device.

```python
import math
import jax
import jax.numpy as jnp
from jax import lax

D = 5120
ZCH = 16
C = 384
STEPS = 50
F = 4
OUTW = 64
HP = 8
WP = 80
SEQ = 2560


def draw_tokens(key, part):
    keys = jax.random.split(jax.random.fold_in(key, 7), 4)
    rows_scale = jnp.exp(jax.random.uniform(keys[0], (SEQ, 1), jnp.float32, 0.0, math.log(10.0)))
    column_scale = jnp.exp(jax.random.uniform(keys[1], (1, D), jnp.float32, 0.0, math.log(10.0)))
    row_centre = jnp.clip(jax.random.normal(keys[2], (SEQ, 1), jnp.float32), -3.0, 3.0)
    basis = jnp.clip(jax.random.normal(keys[3], (SEQ, D), jnp.float32), -6.0, 6.0)
    values = (basis * column_scale + row_centre) * rows_scale
    return values.astype(jnp.bfloat16)


def steps_of(stream_key, shape, cuts, smallest, top_value):
    level = 1.0
    for axis_at, parts in cuts:
        heights = jax.random.uniform(jax.random.fold_in(jax.random.fold_in(stream_key, 6), axis_at), (parts,), jnp.float32, smallest / len(cuts), top_value / len(cuts))
        level = level * jnp.repeat(jnp.exp(heights), shape[axis_at] // parts).reshape((-1,) + (1,) * (len(shape) - 1 - axis_at))
    return level


def bell_draw(key, dims, scale, bound, shards=(), held_as=jnp.bfloat16):
    gain = steps_of(key, dims, shards, -0.22, 0.18) if shards else 1.0
    entries = jax.random.normal(key, dims, jnp.float32) * scale * gain
    return jnp.minimum(jnp.maximum(entries, -bound), bound).astype(held_as)


def setup_inputs(seed: int = 0, part: int = 0) -> dict:
    splits = jax.random.split(jax.random.key(seed), 14)
    own_keys = jax.random.split(jax.random.fold_in(splits[13], part), 14)
    tokens = draw_tokens(jax.random.fold_in(jax.random.fold_in(splits[13], part), 71), part)
    timestep = jax.random.randint(own_keys[1], (1,), 0, STEPS).astype(jnp.int32)
    time_table = bell_draw(splits[2], (STEPS, D), 0.5, 3.0, (), jnp.float32)
    modulation = bell_draw(splits[3], (2, D), 0.5, 3.0, (), jnp.float32)
    head_weight = bell_draw(splits[4], (D, OUTW), D ** -0.5, 0.078125)
    head_bias = bell_draw(splits[5], (OUTW,), 0.5, 3.0, (), jnp.float32)
    latent_std = jnp.clip(jnp.exp(jax.random.uniform(splits[6], (ZCH,), jnp.float32, math.log(0.5), math.log(2.0))), 0.5, 2.0)
    latent_mean = bell_draw(splits[7], (ZCH,), 0.5, 3.0, (), jnp.float32)
    conv_in_weight = bell_draw(splits[8], (27 * ZCH, C), (27 * ZCH) ** -0.5, 0.3125)
    conv_in_bias = bell_draw(splits[9], (C,), 0.5, 3.0, (), jnp.float32)
    norm_gain = jnp.clip(1.0 + 0.18 * jax.random.normal(splits[10], (C,), jnp.float32), 0.1, 1.9)
    conv_weight = bell_draw(splits[11], (27 * C, C), (27 * C) ** -0.5, 0.0625, ((1, 2),))
    conv_bias = bell_draw(splits[12], (C,), 0.5, 3.0, (), jnp.float32)
    return dict(tokens=tokens, timestep=timestep, time_table=time_table, modulation=modulation, head_weight=head_weight, head_bias=head_bias, latent_std=latent_std, latent_mean=latent_mean, conv_in_weight=conv_in_weight, conv_in_bias=conv_in_bias, norm_gain=norm_gain, conv_weight=conv_weight, conv_bias=conv_bias)


def head_latent(tokens, timestep, time_table, modulation, head_weight, head_bias, latent_std, latent_mean):
    select = jnp.arange(time_table.shape[0], dtype=jnp.int32) == timestep[0]
    embed = lax.optimization_barrier(jnp.sum(jnp.where(select[:, None], time_table, jnp.zeros_like(time_table)), axis=0))
    shift_row = modulation[0] + embed
    scale_row = modulation[1] + embed
    values = tokens.astype(jnp.float32)
    centre = lax.optimization_barrier(jnp.mean(values, axis=-1, keepdims=True))
    spread = lax.optimization_barrier(jnp.mean(jnp.square(values - centre), axis=-1, keepdims=True))
    normed = (values - centre) * lax.rsqrt(spread + 1e-06)
    modded = (normed * (1.0 + scale_row) + shift_row).astype(jnp.bfloat16)
    projected = jnp.dot(modded, head_weight, preferred_element_type=jnp.float32) + head_bias
    repeats = head_weight.shape[1] // latent_std.shape[0]
    return (projected * jnp.tile(latent_std, repeats) + jnp.tile(latent_mean, repeats)).astype(jnp.bfloat16)

def unpatch(flattened, frame_count, row_count, col_count, channels):
    blocks = flattened.reshape(frame_count, row_count, col_count, 2, 2, channels)
    blocks = jnp.transpose(blocks, (0, 1, 3, 2, 4, 5))
    return blocks.reshape(frame_count, row_count * 2, col_count * 2, channels)

def conv_input(region, weight, bias):
    frame_count = region.shape[0] - 2
    row_count = region.shape[1] - 2
    col_count = region.shape[2] - 2
    windows = []
    for time_off in range(3):
        for row_off in range(3):
            for col_off in range(3):
                windows.append(region[time_off:time_off + frame_count, row_off:row_off + row_count, col_off:col_off + col_count])
    stacked = jnp.concatenate(windows, axis=-1).reshape(frame_count * row_count * col_count, -1)
    result = jnp.dot(stacked, weight, preferred_element_type=jnp.float32) + bias
    return result.astype(jnp.bfloat16).reshape(frame_count, row_count, col_count, -1)

def activate(block_input, norm_gain):
    values = block_input.astype(jnp.float32)
    factor = lax.rsqrt(lax.optimization_barrier(jnp.mean(values * values, axis=-1, keepdims=True)) + 1e-06)
    return jax.nn.silu(values * factor * norm_gain).astype(jnp.bfloat16)

def conv_taps(padded, weight):
    batches = padded.shape[0]
    frame_count = padded.shape[1] - 2
    row_count = padded.shape[2] - 2
    col_count = padded.shape[3] - 2
    in_width = padded.shape[4]
    running = jnp.zeros((batches * frame_count * row_count * col_count, weight.shape[1]), jnp.float32)
    for kernel_tap in range(27):
        time_off = kernel_tap // 9
        row_off = kernel_tap // 3 % 3
        col_off = kernel_tap % 3
        window = padded[:, time_off:time_off + frame_count, row_off:row_off + row_count, col_off:col_off + col_count].reshape(-1, in_width)
        running = running + jnp.dot(window, weight[kernel_tap * in_width:(kernel_tap + 1) * in_width], preferred_element_type=jnp.float32)
    return running.reshape(batches, frame_count, row_count, col_count, weight.shape[1])

def reference(tokens, timestep, time_table, modulation, head_weight, head_bias, latent_std, latent_mean, conv_in_weight, conv_in_bias, norm_gain, conv_weight, conv_bias):
    latent_rows = head_latent(tokens, timestep, time_table, modulation, head_weight, head_bias, latent_std, latent_mean)
    latent_image = unpatch(latent_rows, F, HP, WP, latent_std.shape[0])
    padded = jnp.pad(latent_image, ((2, 0), (1, 1), (1, 1), (0, 0)))
    block_input = conv_input(padded, conv_in_weight, conv_in_bias)
    activated = activate(block_input, norm_gain)
    act_padded = jnp.pad(activated, ((2, 0), (1, 1), (1, 1), (0, 0)))
    block_mid = (conv_taps(act_padded[None], conv_weight)[0] + conv_bias).astype(jnp.bfloat16)
    return (block_input, block_mid)
```

```python
import functools

import jax
import jax.numpy as jnp
from jax import lax
from jax.experimental import pallas as pl
from jax.experimental.pallas import tpu as pltpu
from jax.sharding import PartitionSpec as P

F = 4
PW = 40
MESH = pl.DeviceIdType.MESH
CP = 96
F32 = jnp.float32
BF16 = jnp.bfloat16
CHUNK = 32


def dot_t(lhs, rhs):
    return lax.dot_general(lhs, rhs, (((1,), (1,)), ((), ())), preferred_element_type=F32)


def kernel(
    heights,
    widths,
    tok_hbm,
    ts_ref,
    table_hbm,
    mod_ref,
    hw_hbm,
    hb_ref,
    std_ref,
    mean_ref,
    ciw_ref,
    cib_ref,
    gain_ref,
    w_hbm,
    cb_ref,
    out1,
    out2,
    tok,
    table,
    hw,
    w,
    modded,
    lat,
    recv,
    zbuf,
    pair,
    wc,
    ybuf,
    xbuf,
    act,
    acc,
    res,
    peer_res,
    stage,
    tok_sem,
    in_sem,
    send_sem,
    recv_sem,
    peer_sem,
):
    ha = lax.axis_index("ha")
    wa = lax.axis_index("wa")
    me = ha * widths + wa
    quarter = heights * widths // F
    frame = me // quarter
    pp = me % quarter
    rows = tok.shape[0]
    cols = rows // 2
    chan = gain_ref.shape[1]
    half_chan = w.shape[0]
    zch = std_ref.shape[1]
    odd = ha % 2

    table_copy = pltpu.make_async_copy(table_hbm, table, in_sem.at[0])
    table_copy.start()

    def tok_copy(i):
        part = pl.ds(pl.multiple_of(i * CHUNK, CHUNK), CHUNK)
        return pltpu.make_async_copy(tok_hbm.at[part], tok.at[part], tok_sem.at[i])

    for i in range(rows // CHUNK):
        tok_copy(i).start()
    hw_copy = pltpu.make_async_copy(hw_hbm, hw, in_sem.at[1])
    hw_copy.start()
    w_copy = pltpu.make_async_copy(w_hbm, w, in_sem.at[2])
    w_copy.start()

    base = ha // 2

    def source(ff, kind):
        if kind == 0:
            return ff * quarter + base, ha >= 0
        return ff * quarter + base + 2 * odd - 1, (ha + 2 * odd - 1 >= 0) & (
            ha + 2 * odd - 1 < heights
        )

    barrier = pltpu.get_barrier_semaphore()
    for ff in range(F):
        for kind in range(2):
            device, exists = source(ff, kind)

            @pl.when(exists & (device != me))
            def _():
                pl.semaphore_signal(
                    barrier,
                    inc=1,
                    device_id={"ha": device // widths, "wa": device % widths},
                    device_id_type=MESH,
                )

    pl.semaphore_signal(barrier, inc=1, device_id={"wa": 1 - wa}, device_id_type=MESH)

    table_copy.wait()
    embed = table[pl.ds(ts_ref[0], 1), :]
    shift = mod_ref[0:1, :] + embed
    scale = 1.0 + (mod_ref[1:2, :] + embed)

    def head_step(i, carry):
        tok_copy(i).wait()
        for j in range(CHUNK // 16):
            part = pl.ds(pl.multiple_of(i * CHUNK + j * 16, 16), 16)
            values = tok[part, :].astype(F32)
            centre = jnp.mean(values, axis=-1, keepdims=True)
            delta = values - centre
            spread = jnp.mean(delta * delta, axis=-1, keepdims=True)
            modded[part, :] = (delta * lax.rsqrt(spread + 1e-06) * scale + shift).astype(BF16)
        return carry

    lax.fori_loop(0, rows // CHUNK, head_step, 0)
    hw_copy.wait()
    projected = dot_t(modded[...], hw[...]) + hb_ref[...]
    repeats = hw.shape[0] // zch
    projected = projected * jnp.concatenate([std_ref[...]] * repeats, axis=1) + jnp.concatenate(
        [mean_ref[...]] * repeats, axis=1
    )
    lat[...] = (
        jnp.concatenate([projected, projected], axis=1).astype(BF16).reshape(2, cols, lat.shape[2])
    )

    plan = ((0, 1, 2, 1), (0, 2, 1, 0), (0, 2, 0, 0), (1, 1, 0, 1))

    def targets():
        for k, (row, count, slot, kind) in enumerate(plan):
            to_ha = 2 * pp - 1 + k
            for to_wa in range(2):
                valid = (to_ha >= 0) & (to_ha < heights)
                mine = (to_ha == ha) & (wa == to_wa)
                copy = pltpu.make_async_remote_copy(
                    src_ref=lat.at[pl.ds(row, count)],
                    dst_ref=recv.at[frame, pl.ds(slot, count)],
                    send_sem=send_sem.at[k, to_wa],
                    recv_sem=recv_sem.at[frame, kind],
                    device_id={"ha": to_ha, "wa": to_wa},
                    device_id_type=MESH,
                )
                yield valid, mine, copy, row, count, slot

    expected = jnp.int32(1)
    for k in range(4):
        to_ha = 2 * pp - 1 + k
        valid = (to_ha >= 0) & (to_ha < heights)
        expected += jnp.where(valid, 2 - jnp.where(to_ha == ha, 1, 0), 0)
    pl.semaphore_wait(barrier, expected)
    for valid, mine, copy, row, count, slot in targets():

        @pl.when(valid & jnp.logical_not(mine))
        def _():
            copy.start()

        @pl.when(valid & mine)
        def _():
            recv[frame, slot : slot + count] = lat[row : row + count]

    wc[...] = jnp.zeros(wc.shape, BF16)
    for a in range(3):
        for win_row in range(4):
            for win_col in range(4):
                k0 = a * 256 + ((win_row // 2) * 2 + win_col // 2) * 64
                k0 += ((win_row % 2) * 2 + win_col % 2) * zch
                for o_row in range(2):
                    for o_col in range(2):
                        b, e = win_row - o_row, win_col - o_col
                        if 0 <= b < 3 and 0 <= e < 3:
                            r0 = ((3 * a + b) * 3 + e) * zch
                            c0 = (o_row * 2 + o_col) * chan
                            wc[k0 : k0 + zch, c0 : c0 + chan] = ciw_ref[r0 : r0 + zch, :]

    @pl.when(ha == 0)
    def _():
        recv[:, 0] = jnp.zeros((F,) + recv.shape[2:], BF16)

    @pl.when(ha == heights - 1)
    def _():
        recv[:, 2] = jnp.zeros((F,) + recv.shape[2:], BF16)

    zbuf[...] = jnp.zeros(zbuf.shape, F32)
    lane = lax.broadcasted_iota(jnp.int32, (CP, 128), 1)
    position = lax.broadcasted_iota(jnp.int32, (88, 1), 0)
    bias_in = jnp.concatenate([cib_ref[...]] * 4, axis=1)
    gain = gain_ref[...]
    first = wa == 0

    for ff in range(F):
        for kind in range(2):
            device, exists = source(ff, kind)
            slot = (1 - odd) if kind == 0 else 2 * odd

            @pl.when(exists & (device != me))
            def _():
                pltpu.make_async_remote_copy(
                    src_ref=lat.at[pl.ds(0, 2 - kind)],
                    dst_ref=recv.at[ff, pl.ds(slot, 2 - kind)],
                    send_sem=send_sem.at[0, 0],
                    recv_sem=recv_sem.at[ff, kind],
                    device_id={"wa": 1 - wa},
                    device_id_type=MESH,
                ).wait_recv()

        for t in range(3):
            zbuf[8 : 8 + cols, :] = recv[ff, t].astype(F32)
            left = zbuf[7 : 7 + CP, :]
            right = zbuf[8 : 8 + CP, :]
            pair[ff, t] = jnp.where(lane < 64, left, right).astype(BF16)

        pieces = []
        for a in range(max(0, 2 - ff), 3):
            for ti in range(2):
                pieces.append(pair[ff + a - 2, ti : ti + 2].reshape(2 * CP, 128))
        lhs = jnp.concatenate(pieces, axis=1)
        ybuf[...] = (
            (
                jnp.dot(lhs, wc[wc.shape[0] - lhs.shape[1] :, :], preferred_element_type=F32)
                + bias_in
            )
            .astype(BF16)
            .astype(F32)
        )
        for i in range(2):
            for o_row in range(2):
                row = 2 * i + o_row
                for o_col in range(2):
                    c0 = (o_row * 2 + o_col) * chan
                    v = ybuf[i * CP : i * CP + 88, c0 : c0 + chan]
                    factor = lax.rsqrt(jnp.mean(v * v, axis=-1, keepdims=True) + 1e-06)
                    z = v * factor * gain
                    s = z / (1.0 + jnp.exp(-z))
                    keep = (position > 0) if o_col == 0 else (position < cols)
                    if row == 0:
                        keep = keep & (ha > 0)
                    if row == 3:
                        keep = keep & (ha < heights - 1)
                    xbuf[o_col] = jnp.where(keep, s, 0.0)
                for h in range(2):
                    lo = h * PW
                    x0 = xbuf[0, lo : lo + PW, :]
                    x1 = xbuf[1, lo : lo + PW, :]
                    x0s = xbuf[0, lo + 1 : lo + 1 + PW, :]
                    x1s = xbuf[1, lo + 1 : lo + 1 + PW, :]
                    act[ff, row, h, :, 0:chan] = jnp.concatenate([x0, x1], axis=0).astype(BF16)
                    act[ff, row, h, :, chan : 2 * chan] = jnp.concatenate(
                        [x1, x0s], axis=0
                    ).astype(BF16)
                    act[ff, row, h, :, 2 * chan : 3 * chan] = jnp.concatenate(
                        [x0s, x1s], axis=0
                    ).astype(BF16)
                if row in (1, 2):
                    c0 = o_row * 2 * chan
                    c1 = c0 + chan
                    r0 = i * CP
                    even = jnp.where(
                        first, ybuf[r0 : r0 + PW, c1 : c1 + chan], ybuf[r0 + PW : r0 + 2 * PW, c1 : c1 + chan]
                    )
                    after = jnp.where(
                        first,
                        ybuf[r0 + 1 : r0 + 1 + PW, c0:c1],
                        ybuf[r0 + 1 + PW : r0 + 1 + 2 * PW, c0:c1],
                    )
                    for q in range(chan // 128):
                        part = slice(q * 128, q * 128 + 128)
                        stage[q, pl.ds(0, PW, stride=2), :] = even[:, part]
                        stage[q, pl.ds(1, PW, stride=2), :] = after[:, part]
                        out1[ff, row - 1, :, part] = stage[q].astype(BF16)

    for valid, mine, copy, row, count, slot in targets():

        @pl.when(valid & jnp.logical_not(mine))
        def _():
            copy.wait_send()

    w_copy.wait()
    bias = jnp.where(first, cb_ref[:, 0:half_chan], cb_ref[:, half_chan : 2 * half_chan])
    peer_copy = pltpu.make_async_remote_copy(
        src_ref=res.at[0],
        dst_ref=peer_res,
        send_sem=peer_sem.at[0],
        recv_sem=peer_sem.at[1],
        device_id={"wa": 1 - wa},
        device_id_type=MESH,
    )

    depth = 3 * chan
    block = 2 * 2 * PW

    def half_step(step, carry):
        h = jnp.where(step == 0, 1 - wa, wa)
        for a in (2, 1, 0):
            frames = 2 + a
            for b in range(3):
                lhs = act[0:frames, b : b + 2, h].reshape(frames * block, depth)
                k0 = (3 * a + b) * depth
                term = dot_t(lhs, w[:, k0 : k0 + depth])
                if a == 2 and b == 0:
                    acc[...] = term
                else:
                    acc[(F - frames) * block :, :] += term
        res[step] = (acc[...] + bias).astype(BF16).reshape(res.shape[1:])

        @pl.when(step == 0)
        def _():
            peer_copy.start()

        return carry

    lax.fori_loop(0, 2, half_step, 0)
    peer_copy.wait()
    for ff in range(F):
        for row in range(2):
            own = res[1, ff, row].astype(F32)
            other = peer_res[ff, row].astype(F32)
            full = jnp.concatenate(
                [jnp.where(first, own, other), jnp.where(first, other, own)], axis=1
            )
            for q in range(chan // 128):
                part = slice(q * 128, q * 128 + 128)
                stage[q, pl.ds(0, PW, stride=2), :] = full[0:PW, part]
                stage[q, pl.ds(1, PW, stride=2), :] = full[PW : 2 * PW, part]
                out2[ff, row, :, part] = stage[q].astype(BF16)


def shards(
    tokens,
    timestep,
    time_table,
    modulation,
    head_weight,
    head_bias,
    latent_std,
    latent_mean,
    conv_in_weight,
    conv_in_bias,
    norm_gain,
    conv_weight,
    conv_bias,
):
    heights = lax.axis_size("ha")
    widths = lax.axis_size("wa")
    rows, width = tokens.shape
    cols = rows // 2
    chan = norm_gain.shape[0]
    half_chan = conv_weight.shape[1]
    whole = pl.BlockSpec(memory_space=pltpu.VMEM)
    far = pl.BlockSpec(memory_space=pl.ANY)
    out = jax.ShapeDtypeStruct((F, 2, 2 * PW, chan), BF16)
    return tuple(
        pl.pallas_call(
            functools.partial(kernel, heights, widths),
            out_shape=(out, out),
            in_specs=[
                far,
                pl.BlockSpec(memory_space=pltpu.SMEM),
                far,
                whole,
                far,
                whole,
                whole,
                whole,
                whole,
                whole,
                whole,
                far,
                whole,
            ],
            out_specs=(whole, whole),
            scratch_shapes=[
                pltpu.VMEM((rows, width), BF16),
                pltpu.VMEM(time_table.shape, F32),
                pltpu.VMEM(head_weight.shape[::-1], BF16),
                pltpu.VMEM(conv_weight.shape[::-1], BF16),
                pltpu.VMEM((rows, width), BF16),
                pltpu.VMEM((2, cols, 128), BF16),
                pltpu.VMEM((F, 3, cols, 128), BF16),
                pltpu.VMEM((CP + 16, 128), F32),
                pltpu.VMEM((F, 3, CP, 128), BF16),
                pltpu.VMEM((768, 4 * chan), BF16),
                pltpu.VMEM((2 * CP, 4 * chan), F32),
                pltpu.VMEM((2, 88, chan), F32),
                pltpu.VMEM((F, 4, 2, 2 * PW, 3 * chan), BF16),
                pltpu.VMEM((F * 4 * PW, half_chan), F32),
                pltpu.VMEM((2, F, 2, 2 * PW, half_chan), BF16),
                pltpu.VMEM((F, 2, 2 * PW, half_chan), BF16),
                pltpu.VMEM((chan // 128, 2 * PW, 128), F32),
                pltpu.SemaphoreType.DMA((rows // CHUNK,)),
                pltpu.SemaphoreType.DMA((3,)),
                pltpu.SemaphoreType.DMA((4, 2)),
                pltpu.SemaphoreType.DMA((F, 2)),
                pltpu.SemaphoreType.DMA((2,)),
            ],
            compiler_params=pltpu.CompilerParams(
                collective_id=0, has_side_effects=True, vmem_limit_bytes=50 << 20
            ),
        )(
            tokens,
            timestep,
            time_table,
            modulation,
            head_weight.T,
            head_bias[None],
            latent_std[None],
            latent_mean[None],
            conv_in_weight,
            conv_in_bias[None],
            norm_gain[None],
            conv_weight.T,
            conv_bias[None],
        )
    )


def solution(mesh):
    in_specs = (
        P(("clips", "ha", "wa"), None),
        P("clips"),
        P(),
        P(),
        P(),
        P(),
        P(),
        P(),
        P(),
        P(),
        P(),
        P(None, "wa"),
        P(),
    )
    out_specs = (P("clips", "ha", "wa", None), P("clips", "ha", "wa", None))
    return jax.shard_map(shards, mesh=mesh, in_specs=in_specs, out_specs=out_specs, check_vma=False)
```

```python
import functools

import jax
import jax.numpy as jnp
from jax import lax
from jax.experimental import pallas as pl
from jax.experimental.pallas import tpu as pltpu
from jax.sharding import PartitionSpec as P

F = 4
PW = 40
MESH = pl.DeviceIdType.MESH
CP = 96
F32 = jnp.float32
BF16 = jnp.bfloat16
CHUNK = 32


def dot_t(lhs, rhs):
    return lax.dot_general(lhs, rhs, (((1,), (1,)), ((), ())), preferred_element_type=F32)


def kernel(
    heights,
    widths,
    tok_hbm,
    ts_hbm,
    table_hbm,
    mod_hbm,
    hw_hbm,
    hb_hbm,
    std_hbm,
    mean_hbm,
    ciw_hbm,
    cib_hbm,
    gain_hbm,
    w_hbm,
    cb_hbm,
    out1,
    out2,
    tok,
    ts_ref,
    table_ref,
    mod_ref,
    hw_ref,
    hb_ref,
    std_ref,
    mean_ref,
    ciw_ref,
    cib_ref,
    gain_ref,
    w_ref,
    cb_ref,
    modded,
    lat,
    recv,
    zbuf,
    pair,
    wc,
    ybuf,
    xbuf,
    act,
    acc,
    res,
    peer_res,
    stage,
    tok_sem,
    in_sem,
    send_sem,
    recv_sem,
    fwd_sem,
    peer_sem,
):
    ha = lax.axis_index("ha")
    wa = lax.axis_index("wa")
    me = ha * widths + wa
    quarter = heights * widths // F
    frame = me // quarter
    pp = me % quarter
    rows = tok.shape[0]
    cols = rows // 2
    chan = gain_ref.shape[1]
    half_chan = w_ref.shape[0]
    zch = std_ref.shape[1]
    odd = ha % 2

    def tok_copy(i):
        part = pl.ds(pl.multiple_of(i * CHUNK, CHUNK), CHUNK)
        return pltpu.make_async_copy(tok_hbm.at[part], tok.at[part], tok_sem.at[i])

    ts_copy = pltpu.make_async_copy(ts_hbm, ts_ref, in_sem.at[0])
    table_copy = pltpu.make_async_copy(table_hbm, table_ref, in_sem.at[1])
    mod_copy = pltpu.make_async_copy(mod_hbm, mod_ref, in_sem.at[2])
    hw_copy = pltpu.make_async_copy(hw_hbm, hw_ref, in_sem.at[3])
    hb_copy = pltpu.make_async_copy(hb_hbm, hb_ref.at[0], in_sem.at[4])
    std_copy = pltpu.make_async_copy(std_hbm, std_ref.at[0], in_sem.at[5])
    mean_copy = pltpu.make_async_copy(mean_hbm, mean_ref.at[0], in_sem.at[6])
    ciw_copy = pltpu.make_async_copy(ciw_hbm, ciw_ref, in_sem.at[7])
    cib_copy = pltpu.make_async_copy(cib_hbm, cib_ref.at[0], in_sem.at[8])
    gain_copy = pltpu.make_async_copy(gain_hbm, gain_ref.at[0], in_sem.at[9])
    cb_copy = pltpu.make_async_copy(cb_hbm, cb_ref.at[0], in_sem.at[10])
    w_copy = pltpu.make_async_copy(w_hbm, w_ref, in_sem.at[11])
    ts_copy.start()
    mod_copy.start()
    table_copy.start()
    for i in range(rows // CHUNK):
        tok_copy(i).start()
    for copy in (hw_copy, hb_copy, std_copy, mean_copy):
        copy.start()
    for copy in (ciw_copy, cib_copy, gain_copy, cb_copy, w_copy):
        copy.start()

    base = ha // 2

    def source(ff, kind):
        if kind == 0:
            return ff * quarter + base, ha >= 0
        return ff * quarter + base + 2 * odd - 1, (ha + 2 * odd - 1 >= 0) & (
            ha + 2 * odd - 1 < heights
        )

    for ff in range(F):
        for edge, slot in ((0, 0), (heights - 1, 2)):

            @pl.when((ha == edge) & (wa == ff % 2))
            def _():
                recv[ff, slot] = jnp.zeros(recv.shape[2:], BF16)

    barrier = pltpu.get_barrier_semaphore()
    for ff in range(F):
        for kind in range(2):
            device, exists = source(ff, kind)

            @pl.when(exists & (device != me) & (wa == ff % 2))
            def _():
                pl.semaphore_signal(
                    barrier,
                    inc=1,
                    device_id={"ha": device // widths, "wa": device % widths},
                    device_id_type=MESH,
                )

    pl.semaphore_signal(barrier, inc=1, device_id={"wa": 1 - wa}, device_id_type=MESH)

    ts_copy.wait()
    mod_copy.wait()
    table_copy.wait()
    embed = table_ref[pl.ds(ts_ref[0], 1), :]
    shift = mod_ref[0:1, :] + embed
    scale = 1.0 + (mod_ref[1:2, :] + embed)

    def head_step(i, carry):
        tok_copy(i).wait()
        for j in range(CHUNK // 16):
            part = pl.ds(pl.multiple_of(i * CHUNK + j * 16, 16), 16)
            values = tok[part, :].astype(F32)
            centre = jnp.mean(values, axis=-1, keepdims=True)
            delta = values - centre
            spread = jnp.mean(delta * delta, axis=-1, keepdims=True)
            modded[part, :] = (delta * lax.rsqrt(spread + 1e-06) * scale + shift).astype(BF16)
        return carry

    lax.fori_loop(0, rows // CHUNK, head_step, 0)
    for copy in (hw_copy, hb_copy, std_copy, mean_copy):
        copy.wait()
    projected = dot_t(modded[...], hw_ref[...]) + hb_ref[...]
    repeats = hw_ref.shape[0] // zch
    projected = projected * jnp.concatenate([std_ref[...]] * repeats, axis=1) + jnp.concatenate(
        [mean_ref[...]] * repeats, axis=1
    )
    for j in range(2):
        both = [projected[j * cols + h * PW : j * cols + (h + 1) * PW] for h in range(2)]
        dense = jnp.concatenate(both, axis=1)
        filler = jnp.zeros((lat.shape[1] - PW, 128), F32)
        lat[j] = jnp.concatenate([dense, filler], axis=0).astype(BF16)

    plan = ((0, 1, 2, 1), (0, 2, 1, 0), (0, 2, 0, 0), (1, 1, 0, 1))

    to_wa = frame % 2

    def targets():
        for k, (row, count, slot, kind) in enumerate(plan):
            to_ha = 2 * pp - 1 + k
            valid = (to_ha >= 0) & (to_ha < heights)
            mine = (to_ha == ha) & (wa == to_wa)
            copy = pltpu.make_async_remote_copy(
                src_ref=lat.at[pl.ds(row, count)],
                dst_ref=recv.at[frame, pl.ds(slot, count)],
                send_sem=send_sem.at[k],
                recv_sem=recv_sem.at[frame, kind],
                device_id={"ha": to_ha, "wa": to_wa},
                device_id_type=MESH,
            )
            yield valid, mine, copy, row, count, slot

    expected = jnp.int32(1)
    for k in range(4):
        to_ha = 2 * pp - 1 + k
        valid = (to_ha >= 0) & (to_ha < heights)
        mine = (to_ha == ha) & (wa == to_wa)
        expected += jnp.where(valid & jnp.logical_not(mine), 1, 0)
    pl.semaphore_wait(barrier, expected)
    for valid, mine, copy, row, count, slot in targets():

        @pl.when(valid & jnp.logical_not(mine))
        def _():
            copy.start()

        @pl.when(valid & mine)
        def _():
            recv[frame, slot : slot + count] = lat[row : row + count]

    for copy in (ciw_copy, cib_copy, gain_copy, cb_copy):
        copy.wait()
    wc[...] = jnp.zeros(wc.shape, BF16)
    for a in range(3):
        for win_row in range(4):
            for win_col in range(4):
                k0 = a * 256 + ((win_row // 2) * 2 + win_col // 2) * 64
                k0 += ((win_row % 2) * 2 + win_col % 2) * zch
                for o_row in range(2):
                    for o_col in range(2):
                        b, e = win_row - o_row, win_col - o_col
                        if 0 <= b < 3 and 0 <= e < 3:
                            r0 = ((3 * a + b) * 3 + e) * zch
                            c0 = (o_row * 2 + o_col) * chan
                            wc[k0 : k0 + zch, c0 : c0 + chan] = ciw_ref[r0 : r0 + zch, :]

    zbuf[...] = jnp.zeros(zbuf.shape, F32)
    lane = lax.broadcasted_iota(jnp.int32, (CP, 128), 1)
    position = lax.broadcasted_iota(jnp.int32, (88, 1), 0)
    bias_in = jnp.concatenate([cib_ref[...]] * 4, axis=1)
    gain = gain_ref[...]
    first = wa == 0

    def forward(ff):
        return pltpu.make_async_remote_copy(
            src_ref=recv.at[ff],
            dst_ref=recv.at[ff],
            send_sem=fwd_sem.at[0, ff],
            recv_sem=fwd_sem.at[1, ff],
            device_id={"wa": 1 - wa},
            device_id_type=MESH,
        )

    for ff in range(F):
        for kind in range(2):
            device, exists = source(ff, kind)
            slot = (1 - odd) if kind == 0 else 2 * odd

            @pl.when(exists & (device != me) & (wa == ff % 2))
            def _():
                pltpu.make_async_remote_copy(
                    src_ref=lat.at[pl.ds(0, 2 - kind)],
                    dst_ref=recv.at[ff, pl.ds(slot, 2 - kind)],
                    send_sem=send_sem.at[0],
                    recv_sem=recv_sem.at[ff, kind],
                    device_id={"wa": 1 - wa},
                    device_id_type=MESH,
                ).wait_recv()

        @pl.when(wa == ff % 2)
        def _():
            forward(ff).start()

    for ff in range(F):

        @pl.when(wa != ff % 2)
        def _():
            forward(ff).wait_recv()

        for t in range(3):
            dense = recv[ff, t].astype(F32)[0:PW]
            swapped = jnp.concatenate([dense[:, 64:128], dense[:, 0:64]], axis=1)
            zbuf[8 : 8 + PW, :] = jnp.where(lane[0:PW] < 64, dense, swapped)
            zbuf[8 + PW : 8 + 2 * PW, :] = jnp.where(lane[0:PW] < 64, swapped, dense)
            left = zbuf[7 : 7 + CP, :]
            right = zbuf[8 : 8 + CP, :]
            pair[ff, t] = jnp.where(lane < 64, left, right).astype(BF16)

        pieces = []
        for a in range(max(0, 2 - ff), 3):
            for ti in range(2):
                pieces.append(pair[ff + a - 2, ti : ti + 2].reshape(2 * CP, 128))
        lhs = jnp.concatenate(pieces, axis=1)
        ybuf[...] = (
            (
                jnp.dot(lhs, wc[wc.shape[0] - lhs.shape[1] :, :], preferred_element_type=F32)
                + bias_in
            )
            .astype(BF16)
            .astype(F32)
        )
        for i in range(2):
            for o_row in range(2):
                row = 2 * i + o_row
                for o_col in range(2):
                    c0 = (o_row * 2 + o_col) * chan
                    v = ybuf[i * CP : i * CP + 88, c0 : c0 + chan]
                    factor = lax.rsqrt(jnp.mean(v * v, axis=-1, keepdims=True) + 1e-06)
                    z = v * factor * gain
                    s = z / (1.0 + jnp.exp(-z))
                    keep = (position > 0) if o_col == 0 else (position < cols)
                    if row == 0:
                        keep = keep & (ha > 0)
                    if row == 3:
                        keep = keep & (ha < heights - 1)
                    xbuf[o_col] = jnp.where(keep, s, 0.0)
                for h in range(2):
                    lo = h * PW
                    x0 = xbuf[0, lo : lo + PW, :]
                    x1 = xbuf[1, lo : lo + PW, :]
                    x0s = xbuf[0, lo + 1 : lo + 1 + PW, :]
                    x1s = xbuf[1, lo + 1 : lo + 1 + PW, :]
                    act[ff, row, h, :, 0:chan] = jnp.concatenate([x0, x1], axis=0).astype(BF16)
                    act[ff, row, h, :, chan : 2 * chan] = jnp.concatenate(
                        [x1, x0s], axis=0
                    ).astype(BF16)
                    act[ff, row, h, :, 2 * chan : 3 * chan] = jnp.concatenate(
                        [x0s, x1s], axis=0
                    ).astype(BF16)
                if row in (1, 2):
                    c0 = o_row * 2 * chan
                    c1 = c0 + chan
                    r0 = i * CP
                    even = jnp.where(
                        first, ybuf[r0 : r0 + PW, c1 : c1 + chan], ybuf[r0 + PW : r0 + 2 * PW, c1 : c1 + chan]
                    )
                    after = jnp.where(
                        first,
                        ybuf[r0 + 1 : r0 + 1 + PW, c0:c1],
                        ybuf[r0 + 1 + PW : r0 + 1 + 2 * PW, c0:c1],
                    )
                    for q in range(chan // 128):
                        part = slice(q * 128, q * 128 + 128)
                        stage[q, pl.ds(0, PW, stride=2), :] = even[:, part]
                        stage[q, pl.ds(1, PW, stride=2), :] = after[:, part]
                        out1[ff, row - 1, :, part] = stage[q].astype(BF16)

    for valid, mine, copy, row, count, slot in targets():

        @pl.when(valid & jnp.logical_not(mine))
        def _():
            copy.wait_send()

    for ff in range(F):

        @pl.when(wa == ff % 2)
        def _():
            forward(ff).wait_send()

    w_copy.wait()
    bias = jnp.where(first, cb_ref[:, 0:half_chan], cb_ref[:, half_chan : 2 * half_chan])
    peer_copy = pltpu.make_async_remote_copy(
        src_ref=res.at[0],
        dst_ref=peer_res,
        send_sem=peer_sem.at[0],
        recv_sem=peer_sem.at[1],
        device_id={"wa": 1 - wa},
        device_id_type=MESH,
    )

    depth = 3 * chan
    block = 2 * 2 * PW

    def half_step(step, carry):
        h = jnp.where(step == 0, 1 - wa, wa)
        for a in (2, 1, 0):
            frames = 2 + a
            for b in range(3):
                lhs = act[0:frames, b : b + 2, h].reshape(frames * block, depth)
                k0 = (3 * a + b) * depth
                term = dot_t(lhs, w_ref[:, k0 : k0 + depth])
                if a == 2 and b == 0:
                    acc[...] = term
                else:
                    acc[(F - frames) * block :, :] += term
        res[step] = (acc[...] + bias).astype(BF16).reshape(res.shape[1:])

        @pl.when(step == 0)
        def _():
            peer_copy.start()

        return carry

    lax.fori_loop(0, 2, half_step, 0)
    peer_copy.wait()
    for ff in range(F):
        for row in range(2):
            own = res[1, ff, row].astype(F32)
            other = peer_res[ff, row].astype(F32)
            full = jnp.concatenate(
                [jnp.where(first, own, other), jnp.where(first, other, own)], axis=1
            )
            for q in range(chan // 128):
                part = slice(q * 128, q * 128 + 128)
                stage[q, pl.ds(0, PW, stride=2), :] = full[0:PW, part]
                stage[q, pl.ds(1, PW, stride=2), :] = full[PW : 2 * PW, part]
                out2[ff, row, :, part] = stage[q].astype(BF16)


def shards(
    tokens,
    timestep,
    time_table,
    modulation,
    head_weight,
    head_bias,
    latent_std,
    latent_mean,
    conv_in_weight,
    conv_in_bias,
    norm_gain,
    conv_weight,
    conv_bias,
):
    heights = lax.axis_size("ha")
    widths = lax.axis_size("wa")
    rows, width = tokens.shape
    cols = rows // 2
    chan = norm_gain.shape[0]
    half_chan = conv_weight.shape[1]
    whole = pl.BlockSpec(memory_space=pltpu.VMEM)
    out = jax.ShapeDtypeStruct((F, 2, 2 * PW, chan), BF16)
    return tuple(
        pl.pallas_call(
            functools.partial(kernel, heights, widths),
            out_shape=(out, out),
            in_specs=[pl.BlockSpec(memory_space=pltpu.HBM)] * 13,
            out_specs=(whole, whole),
            scratch_shapes=[
                pltpu.VMEM((rows, width), BF16),
                pltpu.SMEM((1,), jnp.int32),
                pltpu.VMEM(time_table.shape, F32),
                pltpu.VMEM(modulation.shape, F32),
                pltpu.VMEM(head_weight.shape[::-1], BF16),
                pltpu.VMEM((1,) + head_bias.shape, F32),
                pltpu.VMEM((1,) + latent_std.shape, F32),
                pltpu.VMEM((1,) + latent_mean.shape, F32),
                pltpu.VMEM(conv_in_weight.shape, BF16),
                pltpu.VMEM((1, chan), F32),
                pltpu.VMEM((1, chan), F32),
                pltpu.VMEM(conv_weight.shape[::-1], BF16),
                pltpu.VMEM((1, chan), F32),
                pltpu.VMEM((rows, width), BF16),
                pltpu.VMEM((2, 48, 128), BF16),
                pltpu.VMEM((F, 3, 48, 128), BF16),
                pltpu.VMEM((CP + 16, 128), F32),
                pltpu.VMEM((F, 3, CP, 128), BF16),
                pltpu.VMEM((768, 4 * chan), BF16),
                pltpu.VMEM((2 * CP, 4 * chan), F32),
                pltpu.VMEM((2, 88, chan), F32),
                pltpu.VMEM((F, 4, 2, 2 * PW, 3 * chan), BF16),
                pltpu.VMEM((F * 4 * PW, half_chan), F32),
                pltpu.VMEM((2, F, 2, 2 * PW, half_chan), BF16),
                pltpu.VMEM((F, 2, 2 * PW, half_chan), BF16),
                pltpu.VMEM((chan // 128, 2 * PW, 128), F32),
                pltpu.SemaphoreType.DMA((rows // CHUNK,)),
                pltpu.SemaphoreType.DMA((12,)),
                pltpu.SemaphoreType.DMA((4,)),
                pltpu.SemaphoreType.DMA((F, 2)),
                pltpu.SemaphoreType.DMA((2, F)),
                pltpu.SemaphoreType.DMA((2,)),
            ],
            compiler_params=pltpu.CompilerParams(
                collective_id=0, has_side_effects=True, vmem_limit_bytes=64 << 20
            ),
        )(
            tokens,
            timestep,
            time_table,
            modulation,
            head_weight.T,
            head_bias,
            latent_std,
            latent_mean,
            conv_in_weight,
            conv_in_bias,
            norm_gain,
            conv_weight.T,
            conv_bias,
        )
    )


def solution(mesh):
    in_specs = (
        P(("clips", "ha", "wa"), None),
        P("clips"),
        P(),
        P(),
        P(),
        P(),
        P(),
        P(),
        P(),
        P(),
        P(),
        P(None, "wa"),
        P(),
    )
    out_specs = (P("clips", "ha", "wa", None), P("clips", "ha", "wa", None))
    return jax.shard_map(shards, mesh=mesh, in_specs=in_specs, out_specs=out_specs, check_vma=False)
```

```python
import functools

import jax
import jax.numpy as jnp
from jax import lax
from jax.experimental import pallas as pl
from jax.experimental.pallas import tpu as pltpu
from jax.sharding import PartitionSpec as P

F = 4
PW = 40
MESH = pl.DeviceIdType.MESH
CP = 96
F32 = jnp.float32
BF16 = jnp.bfloat16
CHUNK = 32


def dot_t(lhs, rhs):
    return lax.dot_general(lhs, rhs, (((1,), (1,)), ((), ())), preferred_element_type=F32)


def kernel(
    heights,
    widths,
    tok_hbm,
    ts_hbm,
    table_hbm,
    mod_hbm,
    hw_hbm,
    hb_hbm,
    std_hbm,
    mean_hbm,
    ciw_hbm,
    cib_hbm,
    gain_hbm,
    w_hbm,
    cb_hbm,
    out1,
    out2,
    tok,
    ts_ref,
    table_ref,
    mod_ref,
    hw_ref,
    hb_ref,
    std_ref,
    mean_ref,
    ciw_ref,
    cib_ref,
    gain_ref,
    w_ref,
    cb_ref,
    modded,
    lat,
    recv,
    zbuf,
    pair,
    wc,
    ybuf,
    xbuf,
    act,
    acc,
    res,
    peer_res,
    stage,
    tok_sem,
    in_sem,
    send_sem,
    recv_sem,
    fwd_sem,
    peer_sem,
):
    ha = lax.axis_index("ha")
    wa = lax.axis_index("wa")
    me = ha * widths + wa
    quarter = heights * widths // F
    frame = me // quarter
    pp = me % quarter
    rows = tok.shape[0]
    cols = rows // 2
    chan = gain_ref.shape[1]
    half_chan = w_ref.shape[0]
    zch = std_ref.shape[1]
    odd = ha % 2

    def tok_copy(i):
        part = pl.ds(pl.multiple_of(i * CHUNK, CHUNK), CHUNK)
        return pltpu.make_async_copy(tok_hbm.at[part], tok.at[part], tok_sem.at[i])

    ts_copy = pltpu.make_async_copy(ts_hbm, ts_ref, in_sem.at[0])
    table_copy = pltpu.make_async_copy(table_hbm, table_ref, in_sem.at[1])
    mod_copy = pltpu.make_async_copy(mod_hbm, mod_ref, in_sem.at[2])
    hw_copy = pltpu.make_async_copy(hw_hbm, hw_ref, in_sem.at[3])
    hb_copy = pltpu.make_async_copy(hb_hbm, hb_ref.at[0], in_sem.at[4])
    std_copy = pltpu.make_async_copy(std_hbm, std_ref.at[0], in_sem.at[5])
    mean_copy = pltpu.make_async_copy(mean_hbm, mean_ref.at[0], in_sem.at[6])
    ciw_copy = pltpu.make_async_copy(ciw_hbm, ciw_ref, in_sem.at[7])
    cib_copy = pltpu.make_async_copy(cib_hbm, cib_ref.at[0], in_sem.at[8])
    gain_copy = pltpu.make_async_copy(gain_hbm, gain_ref.at[0], in_sem.at[9])
    cb_copy = pltpu.make_async_copy(cb_hbm, cb_ref.at[0], in_sem.at[10])
    w_copy = pltpu.make_async_copy(w_hbm, w_ref, in_sem.at[11])
    ts_copy.start()
    mod_copy.start()
    table_copy.start()
    for i in range(rows // CHUNK):
        tok_copy(i).start()
    for copy in (hw_copy, hb_copy, std_copy, mean_copy):
        copy.start()
    for copy in (ciw_copy, cib_copy, gain_copy, cb_copy, w_copy):
        copy.start()

    base = ha // 2

    def source(ff, kind):
        if kind == 0:
            return ff * quarter + base, ha >= 0
        return ff * quarter + base + 2 * odd - 1, (ha + 2 * odd - 1 >= 0) & (
            ha + 2 * odd - 1 < heights
        )

    for ff in range(F):
        for edge, slot in ((0, 0), (heights - 1, 2)):

            @pl.when((ha == edge) & (wa == ff % 2))
            def _():
                recv[ff, slot] = jnp.zeros(recv.shape[2:], BF16)

    barrier = pltpu.get_barrier_semaphore()
    for ff in range(F):
        for kind in range(2):
            device, exists = source(ff, kind)

            @pl.when(exists & (device != me) & (wa == ff % 2))
            def _():
                pl.semaphore_signal(
                    barrier,
                    inc=1,
                    device_id={"ha": device // widths, "wa": device % widths},
                    device_id_type=MESH,
                )

    pl.semaphore_signal(barrier, inc=1, device_id={"wa": 1 - wa}, device_id_type=MESH)

    ts_copy.wait()
    mod_copy.wait()
    table_copy.wait()
    embed = table_ref[pl.ds(ts_ref[0], 1), :]
    shift = mod_ref[0:1, :] + embed
    scale = 1.0 + (mod_ref[1:2, :] + embed)

    def head_step(i, carry):
        tok_copy(i).wait()
        for j in range(CHUNK // 16):
            part = pl.ds(pl.multiple_of(i * CHUNK + j * 16, 16), 16)
            values = tok[part, :].astype(F32)
            centre = jnp.mean(values, axis=-1, keepdims=True)
            delta = values - centre
            spread = jnp.mean(delta * delta, axis=-1, keepdims=True)
            modded[part, :] = (delta * lax.rsqrt(spread + 1e-06) * scale + shift).astype(BF16)
        return carry

    lax.fori_loop(0, rows // CHUNK, head_step, 0)
    for copy in (hw_copy, hb_copy, std_copy, mean_copy):
        copy.wait()
    projected = dot_t(modded[...], hw_ref[...]) + hb_ref[...]
    repeats = hw_ref.shape[0] // zch
    projected = projected * jnp.concatenate([std_ref[...]] * repeats, axis=1) + jnp.concatenate(
        [mean_ref[...]] * repeats, axis=1
    )
    for j in range(2):
        both = [projected[j * cols + h * PW : j * cols + (h + 1) * PW] for h in range(2)]
        dense = jnp.concatenate(both, axis=1)
        filler = jnp.zeros((lat.shape[1] - PW, 128), F32)
        lat[j] = jnp.concatenate([dense, filler], axis=0).astype(BF16)

    plan = ((0, 1, 2, 1), (0, 2, 1, 0), (0, 2, 0, 0), (1, 1, 0, 1))

    to_wa = frame % 2

    def targets():
        for k, (row, count, slot, kind) in enumerate(plan):
            to_ha = 2 * pp - 1 + k
            valid = (to_ha >= 0) & (to_ha < heights)
            mine = (to_ha == ha) & (wa == to_wa)
            copy = pltpu.make_async_remote_copy(
                src_ref=lat.at[pl.ds(row, count)],
                dst_ref=recv.at[frame, pl.ds(slot, count)],
                send_sem=send_sem.at[k],
                recv_sem=recv_sem.at[frame, kind],
                device_id={"ha": to_ha, "wa": to_wa},
                device_id_type=MESH,
            )
            yield valid, mine, copy, row, count, slot

    expected = jnp.int32(1)
    for k in range(4):
        to_ha = 2 * pp - 1 + k
        valid = (to_ha >= 0) & (to_ha < heights)
        mine = (to_ha == ha) & (wa == to_wa)
        expected += jnp.where(valid & jnp.logical_not(mine), 1, 0)
    pl.semaphore_wait(barrier, expected)
    for valid, mine, copy, row, count, slot in targets():

        @pl.when(valid & jnp.logical_not(mine))
        def _():
            copy.start()

        @pl.when(valid & mine)
        def _():
            recv[frame, slot : slot + count] = lat[row : row + count]

    for copy in (ciw_copy, cib_copy, gain_copy, cb_copy):
        copy.wait()
    wc[...] = jnp.zeros(wc.shape, BF16)
    for a in range(3):
        for win_row in range(4):
            for win_col in range(4):
                k0 = a * 256 + ((win_row // 2) * 2 + win_col // 2) * 64
                k0 += ((win_row % 2) * 2 + win_col % 2) * zch
                for o_row in range(2):
                    for o_col in range(2):
                        b, e = win_row - o_row, win_col - o_col
                        if 0 <= b < 3 and 0 <= e < 3:
                            r0 = ((3 * a + b) * 3 + e) * zch
                            c0 = (o_row * 2 + o_col) * chan
                            wc[k0 : k0 + zch, c0 : c0 + chan] = ciw_ref[r0 : r0 + zch, :]

    zbuf[...] = jnp.zeros(zbuf.shape, F32)
    lane = lax.broadcasted_iota(jnp.int32, (CP, 128), 1)
    position = lax.broadcasted_iota(jnp.int32, (88, 1), 0)
    bias_in = jnp.concatenate([cib_ref[...]] * 4, axis=1)
    gain = gain_ref[...]
    first = wa == 0

    def forward(ff):
        return pltpu.make_async_remote_copy(
            src_ref=recv.at[ff],
            dst_ref=recv.at[ff],
            send_sem=fwd_sem.at[0, ff],
            recv_sem=fwd_sem.at[1, ff],
            device_id={"wa": 1 - wa},
            device_id_type=MESH,
        )

    for ff in range(F):
        for kind in range(2):
            device, exists = source(ff, kind)
            slot = (1 - odd) if kind == 0 else 2 * odd

            @pl.when(exists & (device != me) & (wa == ff % 2))
            def _():
                pltpu.make_async_remote_copy(
                    src_ref=lat.at[pl.ds(0, 2 - kind)],
                    dst_ref=recv.at[ff, pl.ds(slot, 2 - kind)],
                    send_sem=send_sem.at[0],
                    recv_sem=recv_sem.at[ff, kind],
                    device_id={"wa": 1 - wa},
                    device_id_type=MESH,
                ).wait_recv()

        @pl.when(wa == ff % 2)
        def _():
            forward(ff).start()

    for ff in range(F):

        @pl.when(wa != ff % 2)
        def _():
            forward(ff).wait_recv()

        for t in range(3):
            dense = recv[ff, t].astype(F32)[0:PW]
            swapped = jnp.concatenate([dense[:, 64:128], dense[:, 0:64]], axis=1)
            zbuf[8 : 8 + PW, :] = jnp.where(lane[0:PW] < 64, dense, swapped)
            zbuf[8 + PW : 8 + 2 * PW, :] = jnp.where(lane[0:PW] < 64, swapped, dense)
            left = zbuf[7 : 7 + CP, :]
            right = zbuf[8 : 8 + CP, :]
            pair[ff, t] = jnp.where(lane < 64, left, right).astype(BF16)

        pieces = []
        for a in range(max(0, 2 - ff), 3):
            for ti in range(2):
                pieces.append(pair[ff + a - 2, ti : ti + 2].reshape(2 * CP, 128))
        lhs = jnp.concatenate(pieces, axis=1)
        ybuf[...] = (
            (
                jnp.dot(lhs, wc[wc.shape[0] - lhs.shape[1] :, :], preferred_element_type=F32)
                + bias_in
            )
            .astype(BF16)
            .astype(F32)
        )
        for i in range(2):
            for o_row in range(2):
                row = 2 * i + o_row
                for o_col in range(2):
                    c0 = (o_row * 2 + o_col) * chan
                    v = ybuf[i * CP : i * CP + 88, c0 : c0 + chan]
                    factor = lax.rsqrt(jnp.mean(v * v, axis=-1, keepdims=True) + 1e-06)
                    z = v * factor * gain
                    s = z / (1.0 + jnp.exp(-z))
                    keep = (position > 0) if o_col == 0 else (position < cols)
                    if row == 0:
                        keep = keep & (ha > 0)
                    if row == 3:
                        keep = keep & (ha < heights - 1)
                    xbuf[o_col] = jnp.where(keep, s, 0.0)
                for h in range(2):
                    lo = h * PW
                    x0 = xbuf[0, lo : lo + PW, :]
                    x1 = xbuf[1, lo : lo + PW, :]
                    x0s = xbuf[0, lo + 1 : lo + 1 + PW, :]
                    x1s = xbuf[1, lo + 1 : lo + 1 + PW, :]
                    act[ff, row, h, :, 0:chan] = jnp.concatenate([x0, x1], axis=0).astype(BF16)
                    act[ff, row, h, :, chan : 2 * chan] = jnp.concatenate(
                        [x1, x0s], axis=0
                    ).astype(BF16)
                    act[ff, row, h, :, 2 * chan : 3 * chan] = jnp.concatenate(
                        [x0s, x1s], axis=0
                    ).astype(BF16)
                if row in (1, 2):
                    c0 = o_row * 2 * chan
                    c1 = c0 + chan
                    r0 = i * CP
                    even = jnp.where(
                        first, ybuf[r0 : r0 + PW, c1 : c1 + chan], ybuf[r0 + PW : r0 + 2 * PW, c1 : c1 + chan]
                    )
                    after = jnp.where(
                        first,
                        ybuf[r0 + 1 : r0 + 1 + PW, c0:c1],
                        ybuf[r0 + 1 + PW : r0 + 1 + 2 * PW, c0:c1],
                    )
                    for q in range(chan // 128):
                        part = slice(q * 128, q * 128 + 128)
                        stage[q, pl.ds(0, PW, stride=2), :] = even[:, part]
                        stage[q, pl.ds(1, PW, stride=2), :] = after[:, part]
                        out1[ff, row - 1, :, part] = stage[q].astype(BF16)

    for valid, mine, copy, row, count, slot in targets():

        @pl.when(valid & jnp.logical_not(mine))
        def _():
            copy.wait_send()

    for ff in range(F):

        @pl.when(wa == ff % 2)
        def _():
            forward(ff).wait_send()

    w_copy.wait()
    bias = jnp.where(first, cb_ref[:, 0:half_chan], cb_ref[:, half_chan : 2 * half_chan])
    peer_copy = pltpu.make_async_remote_copy(
        src_ref=res.at[0],
        dst_ref=peer_res,
        send_sem=peer_sem.at[0],
        recv_sem=peer_sem.at[1],
        device_id={"wa": 1 - wa},
        device_id_type=MESH,
    )

    depth = 3 * chan
    block = 2 * 2 * PW

    def half_step(step, carry):
        h = jnp.where(step == 0, 1 - wa, wa)
        for a in (2, 1, 0):
            frames = 2 + a
            for b in range(3):
                lhs = act[0:frames, b : b + 2, h].reshape(frames * block, depth)
                k0 = (3 * a + b) * depth
                term = dot_t(lhs, w_ref[:, k0 : k0 + depth])
                if a == 2 and b == 0:
                    acc[...] = term
                else:
                    acc[(F - frames) * block :, :] += term
        res[step] = (acc[...] + bias).astype(BF16).reshape(res.shape[1:])

        @pl.when(step == 0)
        def _():
            peer_copy.start()

        return carry

    lax.fori_loop(0, 2, half_step, 0)
    peer_copy.wait()
    for ff in range(F):
        for row in range(2):
            own = res[1, ff, row].astype(F32)
            other = peer_res[ff, row].astype(F32)
            full = jnp.concatenate(
                [jnp.where(first, own, other), jnp.where(first, other, own)], axis=1
            )
            for q in range(chan // 128):
                part = slice(q * 128, q * 128 + 128)
                stage[q, pl.ds(0, PW, stride=2), :] = full[0:PW, part]
                stage[q, pl.ds(1, PW, stride=2), :] = full[PW : 2 * PW, part]
                out2[ff, row, :, part] = stage[q].astype(BF16)


def deliver(in1, in2, out1, out2, sem):
    copies = [
        pltpu.make_async_copy(src.at[ff], dst.at[ff], sem.at[i, ff])
        for i, (src, dst) in enumerate(((in1, out1), (in2, out2)))
        for ff in range(F)
    ]
    for copy in copies:
        copy.start()
    for copy in copies:
        copy.wait()


def shards(
    tokens,
    timestep,
    time_table,
    modulation,
    head_weight,
    head_bias,
    latent_std,
    latent_mean,
    conv_in_weight,
    conv_in_bias,
    norm_gain,
    conv_weight,
    conv_bias,
):
    heights = lax.axis_size("ha")
    widths = lax.axis_size("wa")
    rows, width = tokens.shape
    cols = rows // 2
    chan = norm_gain.shape[0]
    half_chan = conv_weight.shape[1]
    whole = pl.BlockSpec(memory_space=pltpu.VMEM)
    out = jax.ShapeDtypeStruct((F, 2, 2 * PW, chan), BF16)
    results = tuple(
        pl.pallas_call(
            functools.partial(kernel, heights, widths),
            out_shape=(out, out),
            in_specs=[pl.BlockSpec(memory_space=pltpu.HBM)] * 13,
            out_specs=(whole, whole),
            scratch_shapes=[
                pltpu.VMEM((rows, width), BF16),
                pltpu.SMEM((1,), jnp.int32),
                pltpu.VMEM(time_table.shape, F32),
                pltpu.VMEM(modulation.shape, F32),
                pltpu.VMEM(head_weight.shape[::-1], BF16),
                pltpu.VMEM((1,) + head_bias.shape, F32),
                pltpu.VMEM((1,) + latent_std.shape, F32),
                pltpu.VMEM((1,) + latent_mean.shape, F32),
                pltpu.VMEM(conv_in_weight.shape, BF16),
                pltpu.VMEM((1, chan), F32),
                pltpu.VMEM((1, chan), F32),
                pltpu.VMEM(conv_weight.shape[::-1], BF16),
                pltpu.VMEM((1, chan), F32),
                pltpu.VMEM((rows, width), BF16),
                pltpu.VMEM((2, 48, 128), BF16),
                pltpu.VMEM((F, 3, 48, 128), BF16),
                pltpu.VMEM((CP + 16, 128), F32),
                pltpu.VMEM((F, 3, CP, 128), BF16),
                pltpu.VMEM((768, 4 * chan), BF16),
                pltpu.VMEM((2 * CP, 4 * chan), F32),
                pltpu.VMEM((2, 88, chan), F32),
                pltpu.VMEM((F, 4, 2, 2 * PW, 3 * chan), BF16),
                pltpu.VMEM((F * 4 * PW, half_chan), F32),
                pltpu.VMEM((2, F, 2, 2 * PW, half_chan), BF16),
                pltpu.VMEM((F, 2, 2 * PW, half_chan), BF16),
                pltpu.VMEM((chan // 128, 2 * PW, 128), F32),
                pltpu.SemaphoreType.DMA((rows // CHUNK,)),
                pltpu.SemaphoreType.DMA((12,)),
                pltpu.SemaphoreType.DMA((4,)),
                pltpu.SemaphoreType.DMA((F, 2)),
                pltpu.SemaphoreType.DMA((2, F)),
                pltpu.SemaphoreType.DMA((2,)),
            ],
            compiler_params=pltpu.CompilerParams(
                collective_id=0, has_side_effects=True, vmem_limit_bytes=64 << 20
            ),
        )(
            tokens,
            timestep,
            time_table,
            modulation,
            head_weight.T,
            head_bias,
            latent_std,
            latent_mean,
            conv_in_weight,
            conv_in_bias,
            norm_gain,
            conv_weight.T,
            conv_bias,
        )
    )
    far = pl.BlockSpec(memory_space=pltpu.HBM)
    return tuple(
        pl.pallas_call(
            deliver,
            out_shape=(out, out),
            in_specs=[far, far],
            out_specs=(far, far),
            scratch_shapes=[pltpu.SemaphoreType.DMA((2, F))],
        )(*results)
    )


def solution(mesh):
    in_specs = (
        P(("clips", "ha", "wa"), None),
        P("clips"),
        P(),
        P(),
        P(),
        P(),
        P(),
        P(),
        P(),
        P(),
        P(),
        P(None, "wa"),
        P(),
    )
    out_specs = (P("clips", "ha", "wa", None), P("clips", "ha", "wa", None))
    return jax.shard_map(shards, mesh=mesh, in_specs=in_specs, out_specs=out_specs, check_vma=False)
```
